256 devices in a mesh: pair: 64 (over z, x, core), virt: 4 (over y).
Axes of the slice: x: 4, y: 4, z: 8, core: 2. Of those that a mesh axis runs over, the one named last changes fastest.
Arguments:
- amps: bfloat16 [2048, 480, 480], P('pair', 'virt'), may hold values from -6 to 6
- integrals: bfloat16 [2304, 230400], P(None, ('virt', 'pair')), may hold values from -0.01171875 to 0.01171875
- slot_pair: int32 [2048], P('pair'), may hold values from -1 to 1175, as said below
- occ_energy: float32 [48], replicated, may hold values from -1.2 to -0.4
- virt_energy: float32 [48], replicated, may hold values from 0.3 to 1.5
Outputs:
- update: float32 [2048, 48, 48], P('pair', 'virt')
The draws below stay inside these ranges and needn't reach their ends.
Inputs may be any that keep to these rules, and one draw needn't show every extreme that they name: `slot_pair`: each of the 1176 pairs i <= j stands in exactly one slot, -1 marks an empty slot; the 32 slots of one index of pair hold uneven numbers of pairs, and some index has all 32 filled.
All inputs are finite; a program needn't handle non-finite values.
Results may differ from the reference program's by a relative error of at most 0.0003.
Values may be sent and summed in bfloat16 or wider, within the bound.
No kernel may reach another device: no remote copies, remote signals or barrier semaphores. Data moves between devices by JAX's collectives and lax.ppermute only.
A program may use at most 192 MiB of HBM per device.

```python
import jax
import jax.numpy as jnp

NOCC = 48
NVIR = 480
WIN = 48
NPAIRS = 1176
SLOTS = 32
SLOTS_ALL = 2048
WW = 2304
CD = 230400
N_PAIR = 64


def draw_slot_pair(key, part):
    key_order, key_fullest, key_rest = jax.random.split(key, 3)
    shuffled = jax.random.permutation(key_order, NPAIRS).astype(jnp.int32)
    fullest = jax.random.randint(key_fullest, (), 0, N_PAIR).astype(jnp.int32)
    remaining = jax.random.permutation(key_rest, SLOTS_ALL - SLOTS)[:NPAIRS - SLOTS].astype(jnp.int32)
    positions = jnp.where(remaining < fullest * SLOTS, remaining, remaining + SLOTS)
    slots_out = jnp.full((SLOTS_ALL,), -1, jnp.int32)
    slots_out = slots_out.at[fullest * SLOTS + jnp.arange(SLOTS, dtype=jnp.int32)].set(shuffled[:SLOTS])
    slots_out = slots_out.at[positions].set(shuffled[SLOTS:])
    return slots_out


def block_scale(key, shape, shards, low, top_value):
    factor_of = 1.0
    for axis_at, parts in shards:
        heights = jax.random.uniform(jax.random.fold_in(jax.random.fold_in(key, 6), axis_at), (parts,), jnp.float32, low / len(shards), top_value / len(shards))
        factor_of = factor_of * jnp.repeat(jnp.exp(heights), shape[axis_at] // parts).reshape((-1,) + (1,) * (len(shape) - 1 - axis_at))
    return factor_of


def centred(rng, dims, scale, most, shards=(), kind=jnp.bfloat16):
    entries = scale * jax.random.normal(rng, dims, jnp.float32)
    if shards:
        entries = entries * block_scale(rng, dims, shards, -0.22, 0.18)
    return jnp.clip(entries, -most, most).astype(kind)


def setup_inputs(seed: int = 0) -> dict:
    arg_keys = jax.random.split(jax.random.key(seed), 6)
    amps = centred(arg_keys[0], (SLOTS_ALL, NVIR, NVIR), 1.0, 6.0, ((0, 64), (1, 4)))
    integrals = centred(arg_keys[1], (WW, CD), CD ** -0.5, 0.01171875, ((1, 256),))
    slot_pair = draw_slot_pair(jax.random.fold_in(arg_keys[5], 71), 0)
    occ_energy = jnp.clip(jax.random.uniform(arg_keys[3], (NOCC,), jnp.float32, -1.2, -0.4), -1.2, -0.4)
    virt_energy = jnp.clip(jax.random.uniform(arg_keys[4], (WIN,), jnp.float32, 0.3, 1.5), 0.3, 1.5)
    return {"amps": amps, "integrals": integrals, "slot_pair": slot_pair, "occ_energy": occ_energy, "virt_energy": virt_energy}


def pair_energy(slot_pair, occ_energy):
    nocc_count = occ_energy.shape[0]
    orbital = jnp.arange(nocc_count, dtype=jnp.int32)
    starts_row = orbital * nocc_count - orbital * (orbital - 1) // 2
    row_index = jnp.sum((starts_row[None, 1:] <= slot_pair[:, None]).astype(jnp.int32), axis=1)
    same_row = orbital[None, :] == row_index[:, None]
    row_start = jnp.sum(jnp.where(same_row, starts_row[None, :], 0), axis=1).astype(jnp.int32)
    column_index = slot_pair - row_start + row_index
    first_energy = jnp.sum(jnp.where(same_row, occ_energy[None, :], jnp.zeros_like(occ_energy)[None, :]), axis=1)
    same_column = orbital[None, :] == column_index[:, None]
    second_energy = jnp.sum(jnp.where(same_column, occ_energy[None, :], jnp.zeros_like(occ_energy)[None, :]), axis=1)
    return first_energy + second_energy, slot_pair >= 0


def reference(amps, integrals, slot_pair, occ_energy, virt_energy):
    count_all = amps.shape[0]
    window = virt_energy.shape[0]
    ladder = jnp.dot(amps.reshape(count_all, -1), integrals.T, preferred_element_type=jnp.float32)
    ladder = ladder.reshape(count_all, window, window)
    residual = ladder + jnp.transpose(ladder, (0, 2, 1))
    pair_sum, filled = pair_energy(slot_pair, occ_energy)
    denominator = pair_sum[:, None, None] - virt_energy[None, :, None] - virt_energy[None, None, :]
    return jnp.where(filled[:, None, None], residual / denominator, jnp.zeros_like(residual))
```

```python
import jax
import jax.numpy as jnp
import numpy as np
from jax import lax
from jax.experimental import pallas as pl
from jax.experimental.pallas import tpu as pltpu
from jax.sharding import PartitionSpec as P

CHUNK = 8
LANES = 128
BF = jnp.bfloat16
F32 = jnp.float32


def params(mib=60):
    return pltpu.CompilerParams(vmem_limit_bytes=mib * 1024 * 1024)


def pair_energy(slot_pair, occ_energy):
    nocc_count = occ_energy.shape[0]
    orbital = jnp.arange(nocc_count, dtype=jnp.int32)
    starts_row = orbital * nocc_count - orbital * (orbital - 1) // 2
    row_index = jnp.sum((starts_row[None, 1:] <= slot_pair[:, None]).astype(jnp.int32), axis=1)
    same_row = orbital[None, :] == row_index[:, None]
    row_start = jnp.sum(jnp.where(same_row, starts_row[None, :], 0), axis=1)
    column_index = slot_pair - row_start + row_index
    first_energy = jnp.sum(
        jnp.where(same_row, occ_energy[None, :], jnp.zeros_like(occ_energy)[None, :]), axis=1
    )
    same_column = orbital[None, :] == column_index[:, None]
    second_energy = jnp.sum(
        jnp.where(same_column, occ_energy[None, :], jnp.zeros_like(occ_energy)[None, :]), axis=1
    )
    return (first_energy + second_energy, slot_pair >= 0)


def unique_pairs(window):
    a, b = np.triu_indices(window)
    count = -(-a.size // 256) * 256
    one = np.full((1, count), -1, np.int32)
    two = np.full((1, count), -1, np.int32)
    one[0, : a.size] = a * window + b
    two[0, : a.size] = b * window + a
    return one, two


def flatten_kernel(dests, width, tiles, x_ref, o_ref, rows, flat):
    count, inner = x_ref.shape[1], x_ref.shape[2]
    for k in range(0, inner, LANES):
        part = min(LANES, inner - k)
        for s in range(CHUNK):
            rows[k // LANES, pl.ds(s * count, count), :part] = x_ref[s, :, k : k + part].astype(F32)
    for c in range(count):
        for k in range(0, inner, LANES):
            part = min(LANES, inner - k)
            piece = rows[k // LANES, pl.ds(c, CHUNK, stride=count), :]
            flat[:, c * inner + k : c * inner + k + part] = piece[:, :part]
    flat[:, count * inner :] = jnp.zeros((CHUNK, flat.shape[1] - count * inner), F32)
    for q in range(dests):
        for t in range(tiles):
            at = q * width + t * LANES
            o_ref[q, t] = flat[:, at : at + LANES].astype(BF)


def flatten(amps, chunk, dests):
    slots, count, inner = amps.shape
    width = count * inner // dests
    tiles = -(-width // LANES)
    return pl.pallas_call(
        lambda *refs: flatten_kernel(dests, width, tiles, *refs),
        grid=(1,),
        in_specs=[pl.BlockSpec((CHUNK, count, inner), lambda i: (chunk, 0, 0))],
        out_specs=pl.BlockSpec((dests, tiles, CHUNK, LANES), lambda i: (0, 0, 0, 0)),
        out_shape=jax.ShapeDtypeStruct((dests, tiles, CHUNK, LANES), BF),
        scratch_shapes=[
            pltpu.VMEM((-(-inner // LANES), CHUNK * count, LANES), F32),
            pltpu.VMEM((CHUNK, count * inner + 2 * LANES), F32),
        ],
        compiler_params=params(),
        cost_estimate=pl.CostEstimate(flops=0, bytes_accessed=4_000_000, transcendentals=0),
    )(amps)


def fold_kernel(one_ref, two_ref, b_ref, hi_ref, lo_ref):
    width, full = b_ref.shape
    row = lax.broadcasted_iota(jnp.int32, (full, one_ref.shape[1]), 0)
    pick = (row == one_ref[...]).astype(F32) + (row == two_ref[...]).astype(F32)
    both = jnp.dot(b_ref[...], pick.astype(BF), preferred_element_type=F32)
    hi = both.astype(BF)
    rest = hi_ref.shape[0] - width
    hi_ref[:width] = hi
    lo_ref[:width] = (both - hi.astype(F32)).astype(BF)
    hi_ref[width:] = jnp.zeros((rest, hi.shape[1]), BF)
    lo_ref[width:] = jnp.zeros((rest, hi.shape[1]), BF)


def fold(columns, one, two):
    width, full = columns.shape
    padded = -(-width // LANES) * LANES
    count, block = one.shape[1], 256
    return pl.pallas_call(
        fold_kernel,
        grid=(count // block,),
        in_specs=[
            pl.BlockSpec((1, block), lambda i: (0, i)),
            pl.BlockSpec((1, block), lambda i: (0, i)),
            pl.BlockSpec((width, full), lambda i: (0, 0), pipeline_mode=pl.Buffered(1)),
        ],
        out_specs=[pl.BlockSpec((padded, block), lambda i: (0, i))] * 2,
        out_shape=[jax.ShapeDtypeStruct((padded, count), BF)] * 2,
        compiler_params=params(),
        cost_estimate=pl.CostEstimate(
            flops=2 * width * full * count, bytes_accessed=10_000_000, transcendentals=0
        ),
    )(one, two, columns)


def ladder_kernel(x_ref, hi_ref, lo_ref, o_ref):
    group, tiles = x_ref.shape[0], x_ref.shape[1]
    total = None
    for t in range(tiles):
        a = x_ref[:, t].astype(F32).reshape(group * CHUNK, LANES).astype(BF)
        at = pl.ds(t * LANES, LANES)
        part = jnp.dot(a, hi_ref[at, :], preferred_element_type=F32)
        part += jnp.dot(a, lo_ref[at, :], preferred_element_type=F32)
        total = part if total is None else total + part
    o_ref[...] = total.reshape(o_ref.shape)


def ladder(panels, hi, lo):
    dests, tiles = panels.shape[0], panels.shape[1]
    padded, count = hi.shape
    group = 16
    return pl.pallas_call(
        ladder_kernel,
        grid=(dests // group,),
        in_specs=[
            pl.BlockSpec((group, tiles, CHUNK, LANES), lambda i: (i, 0, 0, 0)),
            pl.BlockSpec((padded, count), lambda i: (0, 0), pipeline_mode=pl.Buffered(1)),
            pl.BlockSpec((padded, count), lambda i: (0, 0), pipeline_mode=pl.Buffered(1)),
        ],
        out_specs=pl.BlockSpec((group, CHUNK, count), lambda i: (i, 0, 0)),
        out_shape=jax.ShapeDtypeStruct((dests, CHUNK, count), F32),
        compiler_params=params(),
        cost_estimate=pl.CostEstimate(
            flops=4 * dests * CHUNK * padded * count, bytes_accessed=10_000_000, transcendentals=0
        ),
    )(panels, hi, lo)


def update_kernel(window, g_ref, col_ref, pair_ref, ea_ref, eb_ref, o_ref):
    total = jnp.sum(g_ref[...], axis=0)
    slots, count = total.shape
    hi = total.astype(BF).astype(F32)
    mid = (total - hi).astype(BF).astype(F32)
    low = total - hi - mid
    parts = jnp.concatenate([hi, mid, low], axis=0).astype(BF)
    row = lax.broadcasted_iota(jnp.int32, (count, col_ref.shape[1]), 0)
    pick = (row == col_ref[...]).astype(F32).astype(BF)
    wide = jnp.dot(parts, pick, preferred_element_type=F32)
    residual = wide[:slots] + wide[slots : 2 * slots] + wide[2 * slots :]
    denominator = pair_ref[...] - ea_ref[...] - eb_ref[...]
    o_ref[...] = residual / denominator


def body(amps, integrals, slot_pair, occ_energy, virt_energy):
    slots = amps.shape[0]
    window = virt_energy.shape[0]
    pairs = lax.axis_size("pair")
    local_rows = window // lax.axis_size("virt")
    one, two = unique_pairs(window)
    count = one.shape[1]
    hi, lo = fold(integrals.T, jnp.asarray(one), jnp.asarray(two))
    owned = []
    for chunk in range(slots // CHUNK):
        panels = lax.all_to_all(flatten(amps, chunk, pairs), "pair", 0, 0, tiled=True)
        partial = ladder(panels, hi, lo)
        owned.append(lax.psum_scatter(partial, "pair", scatter_dimension=0, tiled=True))
    mine = jnp.concatenate(owned, axis=0).reshape(slots, count)
    everyone = lax.all_gather(mine, "virt", tiled=False)

    pair_sum, filled = pair_energy(slot_pair, occ_energy)
    first = lax.axis_index("virt") * local_rows
    a = jnp.repeat(first + jnp.arange(local_rows, dtype=jnp.int32), window)
    b = jnp.tile(jnp.arange(window, dtype=jnp.int32), local_rows)
    low, high = jnp.minimum(a, b), jnp.maximum(a, b)
    column = low * window - low * (low - 1) // 2 + high - low
    wide = local_rows * window
    full = -(-wide // LANES) * LANES
    column = jnp.pad(column, (0, full - wide), constant_values=-1)[None]
    local_energy = lax.dynamic_slice_in_dim(virt_energy, first, local_rows)
    ea = jnp.pad(jnp.repeat(local_energy, window), (0, full - wide))[None]
    eb = jnp.pad(jnp.tile(virt_energy, local_rows), (0, full - wide))[None]
    update = pl.pallas_call(
        lambda *refs: update_kernel(window, *refs),
        out_shape=jax.ShapeDtypeStruct((slots, full), F32),
        compiler_params=params(),
    )(everyone, column, pair_sum[:, None], ea, eb)
    update = update[:, :wide].reshape(slots, local_rows, window)
    return jnp.where(filled[:, None, None], update, jnp.zeros_like(update))


def solution(mesh):
    placed = (P("pair", "virt", None), P(None, ("virt", "pair")), P("pair"), P(), P())
    return jax.shard_map(
        body, mesh=mesh, in_specs=placed, out_specs=P("pair", "virt", None), check_vma=False
    )
```

```python
import jax
import jax.numpy as jnp
import numpy as np
from jax import lax
from jax.experimental import pallas as pl
from jax.experimental.pallas import tpu as pltpu
from jax.sharding import Mesh, PartitionSpec as P

ROWS = 8
LEFT = 16
COPIES = 2
LANES = 128
BF = jnp.bfloat16
F32 = jnp.float32


def params(mib=60):
    return pltpu.CompilerParams(vmem_limit_bytes=mib * 1024 * 1024)


def pair_energy(slot_pair, occ_energy):
    nocc_count = occ_energy.shape[0]
    orbital = jnp.arange(nocc_count, dtype=jnp.int32)
    starts_row = orbital * nocc_count - orbital * (orbital - 1) // 2
    row_index = jnp.sum((starts_row[None, 1:] <= slot_pair[:, None]).astype(jnp.int32), axis=1)
    same_row = orbital[None, :] == row_index[:, None]
    row_start = jnp.sum(jnp.where(same_row, starts_row[None, :], 0), axis=1)
    column_index = slot_pair - row_start + row_index
    first_energy = jnp.sum(
        jnp.where(same_row, occ_energy[None, :], jnp.zeros_like(occ_energy)[None, :]), axis=1
    )
    same_column = orbital[None, :] == column_index[:, None]
    second_energy = jnp.sum(
        jnp.where(same_column, occ_energy[None, :], jnp.zeros_like(occ_energy)[None, :]), axis=1
    )
    return (first_energy + second_energy, slot_pair >= 0)


def unique_pairs(window):
    a, b = np.triu_indices(window)
    count = -(-a.size // 256) * 256
    one = np.full((1, count), -1, np.int32)
    two = np.full((1, count), -1, np.int32)
    one[0, : a.size] = a * window + b
    two[0, : a.size] = b * window + a
    return one, two


def flatten_kernel(xs, zs, width, where_ref, x_ref, o_ref, rows, flat):
    parts, count, inner = x_ref.shape[0], x_ref.shape[3], x_ref.shape[4]
    core = where_ref[0]
    for k in range(0, inner, LANES):
        part = min(LANES, inner - k)
        for s in range(ROWS):
            rows[k // LANES, pl.ds(s * count, count), :part] = x_ref[
                lax.rem(where_ref[1] + s // COPIES, parts), 0, s % COPIES, :, k : k + part
            ].astype(F32)
    for c in range(count):
        for k in range(0, inner, LANES):
            part = min(LANES, inner - k)
            piece = rows[k // LANES, pl.ds(c, ROWS, stride=count), :]
            flat[:, c * inner + k : c * inner + k + part] = piece[:, :part]
    flat[:, count * inner :] = jnp.zeros((ROWS, flat.shape[1] - count * inner), F32)
    whole = width // LANES
    main = whole * LANES
    lane = lax.broadcasted_iota(jnp.int32, (ROWS, LANES), 1)
    for z in range(zs):
        for x in range(xs):
            base = (z * xs + x) * 2 * width
            q = x * zs + z
            for half in range(2):
                place = lax.bitwise_xor(core, half) * whole
                for t in range(whole):
                    at = base + half * width + t * LANES
                    o_ref[q, 0, place + t] = flat[:, at : at + LANES].astype(BF)
            low, high = base + main, base + width + main
            own = jnp.where(core == 0, flat[:, low : low + LANES], flat[:, high : high + LANES])
            low, high = low - LEFT, high - LEFT
            other = jnp.where(core == 0, flat[:, high : high + LANES], flat[:, low : low + LANES])
            o_ref[q, 0, 2 * whole] = jnp.where(lane < LEFT, own, other).astype(BF)


def flatten(amps, start, size, where, xs, zs):
    slots, count, inner = amps.shape
    width = count * inner // (xs * zs * 2)
    tiles = width // LANES * 2 + 1
    parts = ROWS // COPIES
    view = amps.reshape(parts, slots // ROWS, COPIES, count, inner)
    return pl.pallas_call(
        lambda *refs: flatten_kernel(xs, zs, width, *refs),
        grid_spec=pltpu.PrefetchScalarGridSpec(
            num_scalar_prefetch=1,
            grid=(size,),
            in_specs=[
                pl.BlockSpec((parts, 1, COPIES, count, inner), lambda i, where: (0, start + i, 0, 0, 0))
            ],
            out_specs=pl.BlockSpec((xs * zs, 1, tiles, ROWS, LANES), lambda i, where: (0, i, 0, 0, 0)),
            scratch_shapes=[
                pltpu.VMEM((-(-inner // LANES), ROWS * count, LANES), F32),
                pltpu.VMEM((ROWS, count * inner + 2 * LANES), F32),
            ],
        ),
        out_shape=jax.ShapeDtypeStruct((xs * zs, size, tiles, ROWS, LANES), BF),
        compiler_params=params(),
        cost_estimate=pl.CostEstimate(flops=0, bytes_accessed=8_000_000, transcendentals=0),
    )(where, view)


def fold_kernel(one_ref, two_ref, b_ref, o_ref):
    width, full = b_ref.shape
    row = lax.broadcasted_iota(jnp.int32, (full, one_ref.shape[1]), 0)
    pick = (row == one_ref[...]).astype(F32) + (row == two_ref[...]).astype(F32)
    both = jnp.dot(b_ref[...], pick.astype(BF), preferred_element_type=F32)
    rest = o_ref.shape[1] - width
    both = jnp.concatenate([both, jnp.zeros((rest, both.shape[1]), F32)], axis=0)
    hi = both.astype(BF)
    o_ref[0] = hi
    o_ref[1] = (both - hi.astype(F32)).astype(BF)


def fold(columns, one, two):
    width, full = columns.shape
    padded = width // LANES * LANES + LEFT
    count, block = one.shape[1], 256
    return pl.pallas_call(
        fold_kernel,
        grid=(count // block,),
        in_specs=[
            pl.BlockSpec((1, block), lambda i: (0, i)),
            pl.BlockSpec((1, block), lambda i: (0, i)),
            pl.BlockSpec((width, full), lambda i: (0, 0), pipeline_mode=pl.Buffered(1)),
        ],
        out_specs=pl.BlockSpec((2, padded, block), lambda i: (0, 0, i)),
        out_shape=jax.ShapeDtypeStruct((2, padded, count), BF),
        compiler_params=params(),
        cost_estimate=pl.CostEstimate(
            flops=2 * width * full * count, bytes_accessed=10_000_000, transcendentals=0
        ),
    )(one, two, columns)


def ladder_kernel(xs, where_ref, x_ref, own_ref, other_ref, *o_refs):
    chips, tiles = x_ref.shape[0], x_ref.shape[2]
    zs = chips // xs
    whole = tiles // 2
    main = whole * LANES
    start = where_ref[2]

    def rows_of(t):
        pieces = []
        for r in range(xs):
            at = pl.ds(lax.rem(start + r, xs) * zs, zs)
            pieces.append(x_ref[at, 0, t].astype(F32).reshape(zs * ROWS, LANES))
        return jnp.concatenate(pieces, axis=0).astype(BF)

    left = jnp.concatenate([rows_of(t) for t in range(whole)], axis=1)
    right = jnp.concatenate([rows_of(whole + t) for t in range(whole)], axis=1)
    rest = rows_of(2 * whole)[:, : 2 * LEFT]
    count, block = own_ref.shape[2], 256
    for n in range(0, count, block):
        at = slice(n, n + block)
        total = jnp.zeros((chips * ROWS, block), F32)
        for part in range(2):
            total += jnp.dot(left, own_ref[part, :main, at], preferred_element_type=F32)
            total += jnp.dot(right, other_ref[part, :main, at], preferred_element_type=F32)
            edge = jnp.concatenate([own_ref[part, main:, at], other_ref[part, main:, at]], axis=0)
            total += jnp.dot(rest, edge, preferred_element_type=F32)
        total = total.reshape(xs, zs, ROWS, block)
        for k, o_ref in enumerate(o_refs):
            o_ref[:, 0, :, :, at] = total[:, :, k * COPIES : (k + 1) * COPIES, :]


def ladder(panels, own, other, where, xs, ys):
    chips, size, tiles = panels.shape[:3]
    zs = chips // xs
    count = own.shape[2]
    once = pl.Buffered(1)
    return pl.pallas_call(
        lambda *refs: ladder_kernel(xs, *refs),
        grid_spec=pltpu.PrefetchScalarGridSpec(
            num_scalar_prefetch=1,
            grid=(size,),
            in_specs=[
                pl.BlockSpec((chips, 1, tiles, ROWS, LANES), lambda i, where: (0, i, 0, 0, 0)),
                pl.BlockSpec(own.shape, lambda i, where: (0, 0, 0), pipeline_mode=once),
                pl.BlockSpec(own.shape, lambda i, where: (0, 0, 0), pipeline_mode=once),
            ],
            out_specs=[
                pl.BlockSpec((xs, 1, zs, COPIES, count), lambda i, where: (0, i, 0, 0, 0))
            ] * ys,
        ),
        out_shape=[jax.ShapeDtypeStruct((xs, size, zs, COPIES, count), F32)] * ys,
        compiler_params=params(),
        cost_estimate=pl.CostEstimate(
            flops=4 * size * chips * ROWS * tiles * LANES * count,
            bytes_accessed=size * 3_000_000 + 9_000_000,
            transcendentals=0,
        ),
    )(where, panels, own, other)


def further(block, axis, hops):
    if hops == 0:
        return block
    size = lax.axis_size(axis)
    return lax.ppermute(block, axis, [(i, (i + hops) % size) for i in range(size)])


def update_kernel(place_ref, g_ref, col_ref, pair_ref, ea_ref, eb_ref, o_ref, slots_of):
    parts, rows, count = g_ref.shape
    for k in range(parts):
        slots_of[lax.rem(place_ref[0] + parts - k, parts)] = g_ref[k]
    total = slots_of[...].reshape(parts * rows, count)
    slots = parts * rows
    hi = total.astype(BF).astype(F32)
    mid = (total - hi).astype(BF).astype(F32)
    low = total - hi - mid
    split = jnp.concatenate([hi, mid, low], axis=0).astype(BF)
    row = lax.broadcasted_iota(jnp.int32, (count, col_ref.shape[1]), 0)
    pick = (row == col_ref[...]).astype(F32).astype(BF)
    wide = jnp.dot(split, pick, preferred_element_type=F32)
    residual = wide[:slots] + wide[slots : 2 * slots] + wide[2 * slots :]
    denominator = pair_ref[...] - ea_ref[...] - eb_ref[...]
    o_ref[...] = residual / denominator


def body(amps, integrals, slot_pair, occ_energy, virt_energy):
    slots = amps.shape[0]
    window = virt_energy.shape[0]
    xs, zs, ys = lax.axis_size("x"), lax.axis_size("z"), lax.axis_size("y")
    local_rows = window // ys
    one, two = unique_pairs(window)
    count = one.shape[1]
    where = jnp.stack([lax.axis_index(axis).astype(jnp.int32) for axis in ("c", "y", "x")])
    place = lax.axis_index("y").astype(jnp.int32)
    own = fold(integrals.T, jnp.asarray(one), jnp.asarray(two))
    other = lax.ppermute(own, "c", [(0, 1), (1, 0)])
    reduced = []
    start = 0
    for size in SIZES:
        flat = flatten(amps, start, size, where, xs, zs)
        start += size
        panels = lax.all_to_all(flat, ("x", "z"), 0, 0, tiled=True)
        partial = ladder(panels, own, other, where, xs, ys)
        partial = [further(block, "y", k) for k, block in enumerate(partial)]
        partial = [sum((block[r] for block in partial[1:]), partial[0][r]) for r in range(xs)]
        partial = [further(block, "x", r) for r, block in enumerate(partial)]
        reduced.append(sum(partial[1:], partial[0]))
    mine = jnp.swapaxes(jnp.concatenate(reduced, axis=0), 0, 1).reshape(zs, slots // ys, count)
    mine = jnp.sum(lax.all_to_all(mine, "z", 0, 0, tiled=True), axis=0)
    everyone = jnp.stack([further(mine, "y", k) for k in range(ys)])

    pair_sum, filled = pair_energy(slot_pair, occ_energy)
    first = place * local_rows
    a = jnp.repeat(first + jnp.arange(local_rows, dtype=jnp.int32), window)
    b = jnp.tile(jnp.arange(window, dtype=jnp.int32), local_rows)
    low, high = jnp.minimum(a, b), jnp.maximum(a, b)
    column = low * window - low * (low - 1) // 2 + high - low
    wide = local_rows * window
    full = -(-wide // LANES) * LANES
    column = jnp.pad(column, (0, full - wide), constant_values=-1)[None]
    local_energy = lax.dynamic_slice_in_dim(virt_energy, first, local_rows)
    ea = jnp.pad(jnp.repeat(local_energy, window), (0, full - wide))[None]
    eb = jnp.pad(jnp.tile(virt_energy, local_rows), (0, full - wide))[None]
    update = pl.pallas_call(
        update_kernel,
        in_specs=[pl.BlockSpec(memory_space=pltpu.SMEM)] + [pl.BlockSpec(memory_space=pltpu.VMEM)] * 5,
        out_shape=jax.ShapeDtypeStruct((slots, full), F32),
        scratch_shapes=[pltpu.VMEM(everyone.shape, F32)],
        compiler_params=params(),
    )(place[None], everyone, column, pair_sum[:, None], ea, eb)
    update = update[:, :wide].reshape(slots, local_rows, window)
    return jnp.where(filled[:, None, None], update, jnp.zeros_like(update))


SIZES = (2, 1, 1)


def solution(mesh):
    grid = Mesh(mesh.devices.reshape(8, 4, 2, mesh.shape["virt"]), ("z", "x", "c", "y"))
    placed = (P(("z", "x", "c"), "y", None), P(None, ("y", "z", "x", "c")), P(("z", "x", "c")), P(), P())
    return jax.shard_map(
        body, mesh=grid, in_specs=placed, out_specs=P(("z", "x", "c"), "y", None), check_vma=False
    )
```

```python
import jax
import jax.numpy as jnp
import numpy as np
from jax import lax
from jax.experimental import pallas as pl
from jax.experimental.pallas import tpu as pltpu
from jax.sharding import Mesh, PartitionSpec as P

ROWS = 8
LEFT = 16
COPIES = 2
LANES = 128
BF = jnp.bfloat16
F32 = jnp.float32


def params(mib=40):
    return pltpu.CompilerParams(vmem_limit_bytes=mib * 1024 * 1024)


def pair_energy(slot_pair, occ_energy):
    nocc_count = occ_energy.shape[0]
    orbital = jnp.arange(nocc_count, dtype=jnp.int32)
    starts_row = orbital * nocc_count - orbital * (orbital - 1) // 2
    row_index = jnp.sum((starts_row[None, 1:] <= slot_pair[:, None]).astype(jnp.int32), axis=1)
    same_row = orbital[None, :] == row_index[:, None]
    row_start = jnp.sum(jnp.where(same_row, starts_row[None, :], 0), axis=1)
    column_index = slot_pair - row_start + row_index
    first_energy = jnp.sum(
        jnp.where(same_row, occ_energy[None, :], jnp.zeros_like(occ_energy)[None, :]), axis=1
    )
    same_column = orbital[None, :] == column_index[:, None]
    second_energy = jnp.sum(
        jnp.where(same_column, occ_energy[None, :], jnp.zeros_like(occ_energy)[None, :]), axis=1
    )
    return (first_energy + second_energy, slot_pair >= 0)


def unique_pairs(window):
    a, b = np.triu_indices(window)
    count = -(-a.size // 256) * 256
    one = np.full((1, count), -1, np.int32)
    two = np.full((1, count), -1, np.int32)
    one[0, : a.size] = a * window + b
    two[0, : a.size] = b * window + a
    return one, two


def flatten_kernel(xs, zs, width, where_ref, x_ref, o_ref, rows, flat):
    parts, count, inner = x_ref.shape[0], x_ref.shape[3], x_ref.shape[4]
    for k in range(0, inner, LANES):
        part = min(LANES, inner - k)
        for s in range(ROWS):
            rows[k // LANES, pl.ds(s * count, count), :part] = x_ref[
                lax.rem(where_ref[1] + s // COPIES, parts), 0, s % COPIES, :, k : k + part
            ].astype(F32)
    for c in range(count):
        for k in range(0, inner, LANES):
            part = min(LANES, inner - k)
            piece = rows[k // LANES, pl.ds(c, ROWS, stride=count), :]
            flat[:, c * inner + k : c * inner + k + part] = piece[:, :part]
    flat[:, count * inner :] = jnp.zeros((ROWS, flat.shape[1] - count * inner), F32)
    whole = width // LANES
    main = whole * LANES
    lane = lax.broadcasted_iota(jnp.int32, (ROWS, LANES), 1)
    for z in range(zs):
        for x in range(xs):
            base = (z * xs + x) * 2 * width
            q = x * zs + z
            for half in range(2):
                for t in range(whole):
                    at = base + half * width + t * LANES
                    o_ref[q, 0, half * whole + t] = flat[:, at : at + LANES].astype(BF)
            low, high = base + main, base + width + main - LEFT
            edge = jnp.where(lane < LEFT, flat[:, low : low + LANES], flat[:, high : high + LANES])
            o_ref[q, 0, 2 * whole] = edge.astype(BF)


def flatten(amps, start, size, where, xs, zs):
    slots, count, inner = amps.shape
    width = count * inner // (xs * zs * 2)
    tiles = width // LANES * 2 + 1
    parts = ROWS // COPIES
    view = amps.reshape(parts, slots // ROWS, COPIES, count, inner)
    return pl.pallas_call(
        lambda *refs: flatten_kernel(xs, zs, width, *refs),
        grid_spec=pltpu.PrefetchScalarGridSpec(
            num_scalar_prefetch=1,
            grid=(size,),
            in_specs=[
                pl.BlockSpec((parts, 1, COPIES, count, inner), lambda i, where: (0, start + i, 0, 0, 0))
            ],
            out_specs=pl.BlockSpec((xs * zs, 1, tiles, ROWS, LANES), lambda i, where: (0, i, 0, 0, 0)),
            scratch_shapes=[
                pltpu.VMEM((-(-inner // LANES), ROWS * count, LANES), F32),
                pltpu.VMEM((ROWS, count * inner + 2 * LANES), F32),
            ],
        ),
        out_shape=jax.ShapeDtypeStruct((xs * zs, size, tiles, ROWS, LANES), BF),
        compiler_params=params(),
        cost_estimate=pl.CostEstimate(flops=0, bytes_accessed=8_000_000, transcendentals=0),
    )(where, view)


def fold_kernel(one_ref, two_ref, b_ref, o_ref):
    width, full = b_ref.shape
    row = lax.broadcasted_iota(jnp.int32, (full, one_ref.shape[1]), 0)
    pick = (row == one_ref[...]).astype(F32) + (row == two_ref[...]).astype(F32)
    both = jnp.dot(b_ref[...], pick.astype(BF), preferred_element_type=F32)
    rest = o_ref.shape[1] - width
    both = jnp.concatenate([both, jnp.zeros((rest, both.shape[1]), F32)], axis=0)
    hi = both.astype(BF)
    o_ref[0] = hi
    o_ref[1] = (both - hi.astype(F32)).astype(BF)


def fold(columns, one, two):
    width, full = columns.shape
    padded = width // LANES * LANES + LEFT
    count, block = one.shape[1], 256
    return pl.pallas_call(
        fold_kernel,
        grid=(count // block,),
        in_specs=[
            pl.BlockSpec((1, block), lambda i: (0, i)),
            pl.BlockSpec((1, block), lambda i: (0, i)),
            pl.BlockSpec((width, full), lambda i: (0, 0), pipeline_mode=pl.Buffered(1)),
        ],
        out_specs=pl.BlockSpec((2, padded, block), lambda i: (0, 0, i)),
        out_shape=jax.ShapeDtypeStruct((2, padded, count), BF),
        compiler_params=params(),
        cost_estimate=pl.CostEstimate(
            flops=2 * width * full * count, bytes_accessed=10_000_000, transcendentals=0
        ),
    )(one, two, columns)


def ladder_kernel(xs, where_ref, x_ref, own_ref, other_ref, *refs):
    o_refs, lhs = refs[:-1], refs[-1]
    chips, tiles = x_ref.shape[0], x_ref.shape[2]
    zs = chips // xs
    whole = tiles // 2
    main = whole * LANES
    core, start = where_ref[0], where_ref[2]
    slab = pl.program_id(1)

    @pl.when(pl.program_id(0) == 0)
    def _():
        for t in range(tiles):
            if t < whole:
                tile = core * whole + t
            elif t < 2 * whole:
                tile = (1 - core) * whole + t - whole
            else:
                tile = t
            for r in range(xs):
                at = pl.ds(lax.rem(start + r, xs) * zs, zs)
                piece = x_ref[at, 0, tile].astype(F32).reshape(zs * ROWS, LANES)
                lhs[slab, r * zs * ROWS : (r + 1) * zs * ROWS, t * LANES : (t + 1) * LANES] = piece.astype(BF)

    total = jnp.zeros((chips * ROWS, own_ref.shape[2]), F32)
    for part in range(2):
        total += jnp.dot(lhs[slab, :, :main], own_ref[part, :main, :], preferred_element_type=F32)
        total += jnp.dot(lhs[slab, :, main : 2 * main], other_ref[part, :main, :], preferred_element_type=F32)
        own, other = own_ref[part, main:, :], other_ref[part, main:, :]
        edge = jnp.where(core == 0, jnp.concatenate([own, other], axis=0), jnp.concatenate([other, own], axis=0))
        total += jnp.dot(lhs[slab, :, 2 * main : 2 * main + 2 * LEFT], edge, preferred_element_type=F32)
    total = total.reshape(xs, zs, ROWS, own_ref.shape[2])
    for k, o_ref in enumerate(o_refs):
        o_ref[:, 0] = total[:, :, k * COPIES : (k + 1) * COPIES, :]


def ladder(panels, own, other, where, xs, ys):
    chips, size, tiles = panels.shape[:3]
    zs = chips // xs
    count, block = own.shape[2], 256
    return pl.pallas_call(
        lambda *refs: ladder_kernel(xs, *refs),
        grid_spec=pltpu.PrefetchScalarGridSpec(
            num_scalar_prefetch=1,
            grid=(count // block, size),
            in_specs=[
                pl.BlockSpec(
                    (chips, 1, tiles, ROWS, LANES),
                    lambda n, i, where: (0, jnp.where(n == 0, i, size - 1), 0, 0, 0),
                ),
                pl.BlockSpec((2, own.shape[1], block), lambda n, i, where: (0, 0, n)),
                pl.BlockSpec((2, own.shape[1], block), lambda n, i, where: (0, 0, n)),
            ],
            out_specs=[
                pl.BlockSpec((xs, 1, zs, COPIES, block), lambda n, i, where: (0, i, 0, 0, n))
            ] * ys,
            scratch_shapes=[pltpu.VMEM((size, chips * ROWS, tiles * LANES), BF)],
        ),
        out_shape=[jax.ShapeDtypeStruct((xs, size, zs, COPIES, count), F32)] * ys,
        compiler_params=params(),
        cost_estimate=pl.CostEstimate(
            flops=4 * size * chips * ROWS * tiles * LANES * count,
            bytes_accessed=size * 3_000_000 + 9_000_000,
            transcendentals=0,
        ),
    )(where, panels, own, other)


def further(block, axis, hops):
    if hops == 0:
        return block
    size = lax.axis_size(axis)
    return lax.ppermute(block, axis, [(i, (i + hops) % size) for i in range(size)])


def update_kernel(place_ref, g_ref, col_ref, pair_ref, ea_ref, eb_ref, o_ref, slots_of):
    parts, rows, count = g_ref.shape
    for k in range(parts):
        slots_of[lax.rem(place_ref[0] + parts - k, parts)] = g_ref[k]
    total = slots_of[...].reshape(parts * rows, count)
    slots = parts * rows
    hi = total.astype(BF).astype(F32)
    mid = (total - hi).astype(BF).astype(F32)
    low = total - hi - mid
    split = jnp.concatenate([hi, mid, low], axis=0).astype(BF)
    row = lax.broadcasted_iota(jnp.int32, (count, col_ref.shape[1]), 0)
    pick = (row == col_ref[...]).astype(F32).astype(BF)
    wide = jnp.dot(split, pick, preferred_element_type=F32)
    residual = wide[:slots] + wide[slots : 2 * slots] + wide[2 * slots :]
    denominator = pair_ref[...] - ea_ref[...] - eb_ref[...]
    o_ref[...] = residual / denominator


def body(amps, integrals, slot_pair, occ_energy, virt_energy):
    slots = amps.shape[0]
    window = virt_energy.shape[0]
    xs, zs, ys = lax.axis_size("x"), lax.axis_size("z"), lax.axis_size("y")
    local_rows = window // ys
    one, two = unique_pairs(window)
    count = one.shape[1]
    where = jnp.stack([lax.axis_index(axis).astype(jnp.int32) for axis in ("c", "y", "x")])
    place = lax.axis_index("y").astype(jnp.int32)
    own = fold(integrals.T, jnp.asarray(one), jnp.asarray(two))
    other = lax.ppermute(own, "c", [(0, 1), (1, 0)])
    reduced = []
    start = 0
    for size in SIZES:
        flat = flatten(amps, start, size, where, xs, zs)
        start += size
        panels = lax.all_to_all(flat, ("x", "z"), 0, 0, tiled=True)
        partial = ladder(panels, own, other, where, xs, ys)
        partial = [further(block, "y", k) for k, block in enumerate(partial)]
        partial = [sum((block[r] for block in partial[1:]), partial[0][r]) for r in range(xs)]
        partial = [further(block, "x", r) for r, block in enumerate(partial)]
        reduced.append(sum(partial[1:], partial[0]))
    mine = jnp.swapaxes(jnp.concatenate(reduced, axis=0), 0, 1).reshape(zs, slots // ys, count)
    mine = jnp.sum(lax.all_to_all(mine, "z", 0, 0, tiled=True), axis=0)
    everyone = jnp.stack([further(mine, "y", k) for k in range(ys)])

    pair_sum, filled = pair_energy(slot_pair, occ_energy)
    first = place * local_rows
    a = jnp.repeat(first + jnp.arange(local_rows, dtype=jnp.int32), window)
    b = jnp.tile(jnp.arange(window, dtype=jnp.int32), local_rows)
    low, high = jnp.minimum(a, b), jnp.maximum(a, b)
    column = low * window - low * (low - 1) // 2 + high - low
    wide = local_rows * window
    full = -(-wide // LANES) * LANES
    column = jnp.pad(column, (0, full - wide), constant_values=-1)[None]
    local_energy = lax.dynamic_slice_in_dim(virt_energy, first, local_rows)
    ea = jnp.pad(jnp.repeat(local_energy, window), (0, full - wide))[None]
    eb = jnp.pad(jnp.tile(virt_energy, local_rows), (0, full - wide))[None]
    update = pl.pallas_call(
        update_kernel,
        in_specs=[pl.BlockSpec(memory_space=pltpu.SMEM)] + [pl.BlockSpec(memory_space=pltpu.VMEM)] * 5,
        out_shape=jax.ShapeDtypeStruct((slots, full), F32),
        scratch_shapes=[pltpu.VMEM(everyone.shape, F32)],
        compiler_params=params(),
    )(place[None], everyone, column, pair_sum[:, None], ea, eb)
    update = update[:, :wide].reshape(slots, local_rows, window)
    return jnp.where(filled[:, None, None], update, jnp.zeros_like(update))


SIZES = (2, 1, 1)


def solution(mesh):
    grid = Mesh(mesh.devices.reshape(8, 4, 2, mesh.shape["virt"]), ("z", "x", "c", "y"))
    placed = (P(("z", "x", "c"), "y", None), P(None, ("y", "z", "x", "c")), P(("z", "x", "c")), P(), P())
    return jax.shard_map(
        body, mesh=grid, in_specs=placed, out_specs=P(("z", "x", "c"), "y", None), check_vma=False
    )
```

```python
import jax
import jax.numpy as jnp
import numpy as np
from jax import lax
from jax.experimental import pallas as pl
from jax.experimental.pallas import tpu as pltpu
from jax.sharding import Mesh, PartitionSpec as P

ROWS = 8
LEFT = 16
COPIES = 2
LANES = 128
BF = jnp.bfloat16
F32 = jnp.float32


def params(mib=40):
    return pltpu.CompilerParams(vmem_limit_bytes=mib * 1024 * 1024)


def pair_energy(slot_pair, occ_energy):
    nocc_count = occ_energy.shape[0]
    orbital = jnp.arange(nocc_count, dtype=jnp.int32)
    starts_row = orbital * nocc_count - orbital * (orbital - 1) // 2
    row_index = jnp.sum((starts_row[None, 1:] <= slot_pair[:, None]).astype(jnp.int32), axis=1)
    same_row = orbital[None, :] == row_index[:, None]
    row_start = jnp.sum(jnp.where(same_row, starts_row[None, :], 0), axis=1)
    column_index = slot_pair - row_start + row_index
    first_energy = jnp.sum(
        jnp.where(same_row, occ_energy[None, :], jnp.zeros_like(occ_energy)[None, :]), axis=1
    )
    same_column = orbital[None, :] == column_index[:, None]
    second_energy = jnp.sum(
        jnp.where(same_column, occ_energy[None, :], jnp.zeros_like(occ_energy)[None, :]), axis=1
    )
    return (first_energy + second_energy, slot_pair >= 0)


def unique_pairs(window):
    a, b = np.triu_indices(window)
    count = -(-a.size // 256) * 256
    one = np.full((1, count), -1, np.int32)
    two = np.full((1, count), -1, np.int32)
    one[0, : a.size] = a * window + b
    two[0, : a.size] = b * window + a
    return one, two


def flatten_kernel(xs, zs, width, where_ref, x_ref, o_ref, rows, flat):
    parts, count, inner = x_ref.shape[0], x_ref.shape[3], x_ref.shape[4]
    for k in range(0, inner, LANES):
        part = min(LANES, inner - k)
        for s in range(ROWS):
            rows[k // LANES, pl.ds(s * count, count), :part] = x_ref[
                lax.rem(where_ref[1] + s // COPIES, parts), 0, s % COPIES, :, k : k + part
            ].astype(F32)
    for c in range(count):
        for k in range(0, inner, LANES):
            part = min(LANES, inner - k)
            piece = rows[k // LANES, pl.ds(c, ROWS, stride=count), :]
            flat[:, c * inner + k : c * inner + k + part] = piece[:, :part]
    flat[:, count * inner :] = jnp.zeros((ROWS, flat.shape[1] - count * inner), F32)
    whole = width // LANES
    main = whole * LANES
    lane = lax.broadcasted_iota(jnp.int32, (ROWS, LANES), 1)
    for z in range(zs):
        for x in range(xs):
            base = (z * xs + x) * 2 * width
            q = x * zs + z
            for half in range(2):
                for t in range(whole):
                    at = base + half * width + t * LANES
                    o_ref[q, 0, half * whole + t] = flat[:, at : at + LANES].astype(BF)
            low, high = base + main, base + width + main - LEFT
            edge = jnp.where(lane < LEFT, flat[:, low : low + LANES], flat[:, high : high + LANES])
            o_ref[q, 0, 2 * whole] = edge.astype(BF)


def flatten(amps, start, size, where, xs, zs):
    slots, count, inner = amps.shape
    width = count * inner // (xs * zs * 2)
    tiles = width // LANES * 2 + 1
    parts = ROWS // COPIES
    view = amps.reshape(parts, slots // ROWS, COPIES, count, inner)
    return pl.pallas_call(
        lambda *refs: flatten_kernel(xs, zs, width, *refs),
        grid_spec=pltpu.PrefetchScalarGridSpec(
            num_scalar_prefetch=1,
            grid=(size,),
            in_specs=[
                pl.BlockSpec((parts, 1, COPIES, count, inner), lambda i, where: (0, start + i, 0, 0, 0))
            ],
            out_specs=pl.BlockSpec((xs * zs, 1, tiles, ROWS, LANES), lambda i, where: (0, i, 0, 0, 0)),
            scratch_shapes=[
                pltpu.VMEM((-(-inner // LANES), ROWS * count, LANES), F32),
                pltpu.VMEM((ROWS, count * inner + 2 * LANES), F32),
            ],
        ),
        out_shape=jax.ShapeDtypeStruct((xs * zs, size, tiles, ROWS, LANES), BF),
        compiler_params=params(),
        cost_estimate=pl.CostEstimate(flops=0, bytes_accessed=8_000_000, transcendentals=0),
    )(where, view)


def fold_kernel(one_ref, two_ref, b_ref, o_ref):
    width, full = b_ref.shape
    row = lax.broadcasted_iota(jnp.int32, (full, one_ref.shape[1]), 0)
    pick = (row == one_ref[...]).astype(F32) + (row == two_ref[...]).astype(F32)
    both = jnp.dot(b_ref[...], pick.astype(BF), preferred_element_type=F32)
    rest = o_ref.shape[2] - width
    both = jnp.concatenate([both, jnp.zeros((rest, both.shape[1]), F32)], axis=0)
    hi = both.astype(BF)
    o_ref[0, 0] = hi
    o_ref[0, 1] = (both - hi.astype(F32)).astype(BF)


def fold(columns, one, two):
    width, full = columns.shape
    padded = width // LANES * LANES + LEFT
    count, block = one.shape[1], 256
    return pl.pallas_call(
        fold_kernel,
        grid=(count // block,),
        in_specs=[
            pl.BlockSpec((1, block), lambda i: (0, i)),
            pl.BlockSpec((1, block), lambda i: (0, i)),
            pl.BlockSpec((width, full), lambda i: (0, 0), pipeline_mode=pl.Buffered(1)),
        ],
        out_specs=pl.BlockSpec((1, 2, padded, block), lambda i: (i, 0, 0, 0)),
        out_shape=jax.ShapeDtypeStruct((count // block, 2, padded, block), BF),
        compiler_params=params(),
        cost_estimate=pl.CostEstimate(
            flops=2 * width * full * count, bytes_accessed=10_000_000, transcendentals=0
        ),
    )(one, two, columns)


def ladder_block(xs, where_ref, x_ref, own_ref, other_ref, lhs):
    chips, size, tiles = x_ref.shape[:3]
    zs = chips // xs
    whole = tiles // 2
    main = whole * LANES
    core = where_ref[0]

    @pl.when(pl.program_id(0) == 0)
    def _():
        for r in range(xs):
            for s in range(zs // 2):
                pick = [
                    lax.rem(where_ref[2] + r, xs) * zs + lax.bitwise_xor(where_ref[3], 2 * s + odd)
                    for odd in range(2)
                ]
                for i in range(size):
                    at = ((i * xs + r) * zs + 2 * s) * ROWS
                    for t in range(tiles):
                        if t < whole:
                            tile = core * whole + t
                        elif t < 2 * whole:
                            tile = (1 - core) * whole + t - whole
                        else:
                            tile = t
                        pair = jnp.concatenate([x_ref[q, i, tile].astype(F32) for q in pick], axis=0)
                        lhs[at : at + 2 * ROWS, t * LANES : (t + 1) * LANES] = pair.astype(BF)

    total = jnp.zeros((lhs.shape[0], own_ref.shape[3]), F32)
    for part in range(2):
        total += jnp.dot(lhs[:, :main], own_ref[0, part, :main], preferred_element_type=F32)
        total += jnp.dot(lhs[:, main : 2 * main], other_ref[0, part, :main], preferred_element_type=F32)
        own, other = own_ref[0, part, main:], other_ref[0, part, main:]
        edge = jnp.where(core == 0, jnp.concatenate([own, other], axis=0), jnp.concatenate([other, own], axis=0))
        total += jnp.dot(lhs[:, 2 * main : 2 * main + 2 * LEFT], edge, preferred_element_type=F32)
    return total


def ladder_kernel(xs, where_ref, x_ref, own_ref, other_ref, *refs):
    o_refs, lhs = refs[:-1], refs[-1]
    total = ladder_block(xs, where_ref, x_ref, own_ref, other_ref, lhs)
    size, zs, block = x_ref.shape[1], x_ref.shape[0] // xs, total.shape[1]
    total = total.reshape(size, xs, zs, ROWS, block)
    at = pl.ds(pl.multiple_of(pl.program_id(0) * block, block), block)
    for k, o_ref in enumerate(o_refs):
        for i in range(size):
            o_ref[:, i, :, :, at] = total[i, :, :, k * COPIES : (k + 1) * COPIES, :]


def whole_kernel(xs, where_ref, x_ref, own_ref, other_ref, o_ref, f_ref, lhs, most):
    total = ladder_block(xs, where_ref, x_ref, own_ref, other_ref, lhs)
    block = total.shape[1]
    total = total.reshape(o_ref.shape[0], ROWS, block)
    step = pl.program_id(0)
    at = pl.ds(pl.multiple_of(step * block, block), block)
    o_ref[:, :, at] = total
    top = jnp.max(jnp.abs(total), axis=0)

    @pl.when(step == 0)
    def _():
        most[...] = top

    @pl.when(step > 0)
    def _():
        most[...] = jnp.maximum(most[...], top)

    @pl.when(step == pl.num_programs(0) - 1)
    def _():
        left = jnp.max(most[...])
        factors, inverses = [], []
        for _ in range(3):
            factor, inverse = jnp.float32(1), jnp.float32(1)
            for power in (7, 4, 2, 1):
                small = left * float(2**power) <= 16384.0
                grow = jnp.where(small, float(2**power), 1.0)
                left, factor = left * grow, factor * grow
                inverse = inverse * jnp.where(small, 2.0**-power, 1.0)
            factors.append(factor)
            inverses.append(inverse)
        lane = lax.broadcasted_iota(jnp.int32, f_ref.shape, 1)
        out = jnp.zeros(f_ref.shape, F32)
        for n, value in enumerate(factors + inverses):
            out = jnp.where(lane == n, value, out)
        f_ref[...] = out


def ladder(panels, own, other, where, xs, ys, whole=False):
    chips, size, tiles = panels.shape[:3]
    zs = chips // xs
    blocks, _, padded, block = own.shape
    count = blocks * block
    scratch = [pltpu.VMEM((size * chips * ROWS, tiles * LANES), BF)]
    if whole:
        shapes = [(chips, ROWS, count), (8, LANES)]
        scratch.append(pltpu.VMEM((ROWS, block), F32))
    else:
        shapes = [(xs, size, zs, COPIES, count)] * ys
    kernel = whole_kernel if whole else ladder_kernel
    return pl.pallas_call(
        lambda *refs: kernel(xs, *refs),
        grid_spec=pltpu.PrefetchScalarGridSpec(
            num_scalar_prefetch=1,
            grid=(blocks,),
            in_specs=[
                pl.BlockSpec(panels.shape, lambda n, where: (0, 0, 0, 0, 0), pipeline_mode=pl.Buffered(1)),
                pl.BlockSpec((1, 2, padded, block), lambda n, where: (n, 0, 0, 0)),
                pl.BlockSpec((1, 2, padded, block), lambda n, where: (n, 0, 0, 0)),
            ],
            out_specs=[pl.BlockSpec(shape, lambda n, where, rank=len(shape): (0,) * rank) for shape in shapes],
            scratch_shapes=scratch,
        ),
        out_shape=[jax.ShapeDtypeStruct(shape, F32) for shape in shapes],
        compiler_params=params(),
        cost_estimate=pl.CostEstimate(
            flops=4 * size * chips * ROWS * tiles * LANES * count,
            bytes_accessed=size * 3_000_000 + 9_000_000,
            transcendentals=0,
        ),
    )(where, panels, own, other)


def encode(partial, factors):
    count = partial.shape[2]
    lane = lax.broadcasted_iota(jnp.int32, partial.shape, 2)
    coded = partial * (factors[0, 0] * factors[0, 1] * factors[0, 2])
    for n in range(3):
        coded = jnp.where(lane == count - 1 - n, factors[0, 3 + n], coded)
    return coded.astype(jnp.float16)


def decode(coded):
    wide = coded.astype(F32)
    count = wide.shape[2]
    inverse = wide[:, :1, count - 1 :] * wide[:, :1, count - 2 : count - 1] * wide[:, :1, count - 3 : count - 2]
    return jnp.sum(wide * inverse, axis=0)


def further(block, axis, hops):
    if hops == 0:
        return block
    size = lax.axis_size(axis)
    return lax.ppermute(block, axis, [(i, (i + hops) % size) for i in range(size)])


def update_kernel(place_ref, g_ref, col_ref, pair_ref, ea_ref, eb_ref, o_ref, slots_of):
    parts, rows, count = slots_of.shape
    done = rows - COPIES
    for k in range(parts):
        slots_of[lax.rem(place_ref[0] + parts - k, parts), :done] = g_ref[k, :done]
    last = g_ref[0, rows:]
    for k in range(1, parts):
        last = last + g_ref[k, rows:]
    for k in range(parts):
        slots_of[k, done:] = last[k * COPIES : (k + 1) * COPIES]
    total = slots_of[...].reshape(parts * rows, count)
    slots = parts * rows
    hi = total.astype(BF).astype(F32)
    mid = (total - hi).astype(BF).astype(F32)
    low = total - hi - mid
    split = jnp.concatenate([hi, mid, low], axis=0).astype(BF)
    row = lax.broadcasted_iota(jnp.int32, (count, col_ref.shape[1]), 0)
    pick = (row == col_ref[...]).astype(F32).astype(BF)
    wide = jnp.dot(split, pick, preferred_element_type=F32)
    residual = wide[:slots] + wide[slots : 2 * slots] + wide[2 * slots :]
    denominator = pair_ref[...] - ea_ref[...] - eb_ref[...]
    o_ref[...] = residual / denominator


def body(amps, integrals, slot_pair, occ_energy, virt_energy):
    slots = amps.shape[0]
    window = virt_energy.shape[0]
    xs, zs, ys = lax.axis_size("x"), lax.axis_size("z"), lax.axis_size("y")
    local_rows = window // ys
    one, two = unique_pairs(window)
    count = one.shape[1]
    where = jnp.stack([lax.axis_index(axis).astype(jnp.int32) for axis in ("c", "y", "x", "z")])
    plain = where * jnp.asarray([1, 0, 0, 0], jnp.int32)
    place = lax.axis_index("y").astype(jnp.int32)
    own = fold(integrals.T, jnp.asarray(one), jnp.asarray(two))
    other = lax.ppermute(own, "c", [(0, 1), (1, 0)])
    done = []
    start = 0
    for chunk, size in enumerate(SIZES):
        final = chunk == len(SIZES) - 1
        flat = flatten(amps, start, size, plain if final else where, xs, zs)
        start += size
        panels = lax.all_to_all(flat, ("x", "z"), 0, 0, tiled=True)
        partial = ladder(panels, own, other, plain if final else where, xs, ys, final)
        if final:
            coded = encode(*partial)
            coded = lax.all_to_all(coded, ("x", "z"), 0, 0, tiled=True)
            last = decode(coded)
            continue
        partial = [further(block, "y", k) for k, block in enumerate(partial)]
        partial = [sum((block[r] for block in partial[1:]), partial[0][r]) for r in range(xs)]
        partial = [further(block, "x", r) for r, block in enumerate(partial)]
        done.append(sum(partial[1:], partial[0]))
    mine = jnp.concatenate(done, axis=0)
    half = zs
    while half > 1:
        half //= 2
        swap = [(i, i ^ half) for i in range(zs)]
        mine = mine[:, :half] + lax.ppermute(mine[:, half:], "z", swap)
    mine = mine.reshape(-1, count)
    mine = jnp.concatenate([jnp.pad(mine, ((0, COPIES), (0, 0))), last], axis=0)
    everyone = jnp.stack([further(mine, "y", k) for k in range(ys)])

    pair_sum, filled = pair_energy(slot_pair, occ_energy)
    first = place * local_rows
    a = jnp.repeat(first + jnp.arange(local_rows, dtype=jnp.int32), window)
    b = jnp.tile(jnp.arange(window, dtype=jnp.int32), local_rows)
    low, high = jnp.minimum(a, b), jnp.maximum(a, b)
    column = low * window - low * (low - 1) // 2 + high - low
    wide = local_rows * window
    full = -(-wide // LANES) * LANES
    column = jnp.pad(column, (0, full - wide), constant_values=-1)[None]
    local_energy = lax.dynamic_slice_in_dim(virt_energy, first, local_rows)
    ea = jnp.pad(jnp.repeat(local_energy, window), (0, full - wide))[None]
    eb = jnp.pad(jnp.tile(virt_energy, local_rows), (0, full - wide))[None]
    update = pl.pallas_call(
        update_kernel,
        in_specs=[pl.BlockSpec(memory_space=pltpu.SMEM)] + [pl.BlockSpec(memory_space=pltpu.VMEM)] * 5,
        out_shape=jax.ShapeDtypeStruct((slots, full), F32),
        scratch_shapes=[pltpu.VMEM((ys, slots // ys, count), F32)],
        compiler_params=params(),
    )(place[None], everyone, column, pair_sum[:, None], ea, eb)
    update = update[:, :wide].reshape(slots, local_rows, window)
    return jnp.where(filled[:, None, None], update, jnp.zeros_like(update))


SIZES = (2, 1, 1)


def solution(mesh):
    grid = Mesh(mesh.devices.reshape(8, 4, 2, mesh.shape["virt"]), ("z", "x", "c", "y"))
    placed = (P(("z", "x", "c"), "y", None), P(None, ("y", "z", "x", "c")), P(("z", "x", "c")), P(), P())
    return jax.shard_map(
        body, mesh=grid, in_specs=placed, out_specs=P(("z", "x", "c"), "y", None), check_vma=False
    )
```

```python
import jax
import jax.numpy as jnp
import numpy as np
from jax import lax
from jax.experimental import pallas as pl
from jax.experimental.pallas import tpu as pltpu
from jax.sharding import Mesh, PartitionSpec as P

ROWS = 8
LEFT = 16
COPIES = 2
LADDER_MIB = 60
LANES = 128
BF = jnp.bfloat16
F32 = jnp.float32


def params(mib):
    return pltpu.CompilerParams(vmem_limit_bytes=mib * 1024 * 1024)


def pair_energy(slot_pair, occ_energy):
    nocc_count = occ_energy.shape[0]
    orbital = jnp.arange(nocc_count, dtype=jnp.int32)
    starts_row = orbital * nocc_count - orbital * (orbital - 1) // 2
    row_index = jnp.sum((starts_row[None, 1:] <= slot_pair[:, None]).astype(jnp.int32), axis=1)
    same_row = orbital[None, :] == row_index[:, None]
    row_start = jnp.sum(jnp.where(same_row, starts_row[None, :], 0), axis=1)
    column_index = slot_pair - row_start + row_index
    first_energy = jnp.sum(
        jnp.where(same_row, occ_energy[None, :], jnp.zeros_like(occ_energy)[None, :]), axis=1
    )
    same_column = orbital[None, :] == column_index[:, None]
    second_energy = jnp.sum(
        jnp.where(same_column, occ_energy[None, :], jnp.zeros_like(occ_energy)[None, :]), axis=1
    )
    return (first_energy + second_energy, slot_pair >= 0)


def unique_pairs(window):
    a, b = np.triu_indices(window)
    count = -(-a.size // 256) * 256
    one = np.full((1, count), -1, np.int32)
    two = np.full((1, count), -1, np.int32)
    one[0, : a.size] = a * window + b
    two[0, : a.size] = b * window + a
    return one, two


def flatten_kernel(xs, zs, width, where_ref, x_ref, o_ref, rows, flat):
    parts, count, inner = x_ref.shape[0], x_ref.shape[3], x_ref.shape[4]
    for k in range(0, inner, LANES):
        part = min(LANES, inner - k)
        for s in range(ROWS):
            rows[k // LANES, pl.ds(s * count, count), :part] = x_ref[
                lax.rem(where_ref[1] + s // COPIES, parts), 0, s % COPIES, :, k : k + part
            ].astype(F32)
    for c in range(count):
        for k in range(0, inner, LANES):
            part = min(LANES, inner - k)
            piece = rows[k // LANES, pl.ds(c, ROWS, stride=count), :]
            flat[:, c * inner + k : c * inner + k + part] = piece[:, :part]
    flat[:, count * inner :] = jnp.zeros((ROWS, flat.shape[1] - count * inner), F32)
    whole = width // LANES
    main = whole * LANES
    lane = lax.broadcasted_iota(jnp.int32, (ROWS, LANES), 1)
    for z in range(zs):
        for x in range(xs):
            base = (z * xs + x) * 2 * width
            q = x * zs + z
            for half in range(2):
                for t in range(whole):
                    at = base + half * width + t * LANES
                    o_ref[q, 0, half * whole + t] = flat[:, at : at + LANES].astype(BF)
            low, high = base + main, base + width + main - LEFT
            edge = jnp.where(lane < LEFT, flat[:, low : low + LANES], flat[:, high : high + LANES])
            o_ref[q, 0, 2 * whole] = edge.astype(BF)


def flatten(amps, start, size, where, xs, zs):
    slots, count, inner = amps.shape
    width = count * inner // (xs * zs * 2)
    tiles = width // LANES * 2 + 1
    parts = ROWS // COPIES
    view = amps.reshape(parts, slots // ROWS, COPIES, count, inner)
    return pl.pallas_call(
        lambda *refs: flatten_kernel(xs, zs, width, *refs),
        grid_spec=pltpu.PrefetchScalarGridSpec(
            num_scalar_prefetch=1,
            grid=(size,),
            in_specs=[
                pl.BlockSpec((parts, 1, COPIES, count, inner), lambda i, where: (0, start + i, 0, 0, 0))
            ],
            out_specs=pl.BlockSpec((xs * zs, 1, tiles, ROWS, LANES), lambda i, where: (0, i, 0, 0, 0)),
            scratch_shapes=[
                pltpu.VMEM((-(-inner // LANES), ROWS * count, LANES), F32),
                pltpu.VMEM((ROWS, count * inner + 2 * LANES), F32),
            ],
        ),
        out_shape=jax.ShapeDtypeStruct((xs * zs, size, tiles, ROWS, LANES), BF),
        compiler_params=params(60),
        cost_estimate=pl.CostEstimate(flops=0, bytes_accessed=8_000_000, transcendentals=0),
    )(where, view)


def fold_kernel(one_ref, two_ref, b_ref, o_ref):
    width, full = b_ref.shape
    row = lax.broadcasted_iota(jnp.int32, (full, one_ref.shape[1]), 0)
    pick = (row == one_ref[...]).astype(F32) + (row == two_ref[...]).astype(F32)
    both = jnp.dot(b_ref[...], pick.astype(BF), preferred_element_type=F32)
    rest = o_ref.shape[2] - width
    both = jnp.concatenate([both, jnp.zeros((rest, both.shape[1]), F32)], axis=0)
    hi = both.astype(BF)
    o_ref[0, 0] = hi
    o_ref[0, 1] = (both - hi.astype(F32)).astype(BF)


def fold(columns, one, two):
    width, full = columns.shape
    padded = width // LANES * LANES + LEFT
    count, block = one.shape[1], 256
    return pl.pallas_call(
        fold_kernel,
        grid=(count // block,),
        in_specs=[
            pl.BlockSpec((1, block), lambda i: (0, i)),
            pl.BlockSpec((1, block), lambda i: (0, i)),
            pl.BlockSpec((width, full), lambda i: (0, 0), pipeline_mode=pl.Buffered(1)),
        ],
        out_specs=pl.BlockSpec((1, 2, padded, block), lambda i: (i, 0, 0, 0)),
        out_shape=jax.ShapeDtypeStruct((count // block, 2, padded, block), BF),
        compiler_params=params(60),
        cost_estimate=pl.CostEstimate(
            flops=2 * width * full * count, bytes_accessed=10_000_000, transcendentals=0
        ),
    )(one, two, columns)


def ladder_block(xs, where_ref, x_ref, own_ref, other_ref, lhs):
    chips, size, tiles = x_ref.shape[:3]
    zs = chips // xs
    whole = tiles // 2
    main = whole * LANES
    core = where_ref[0]

    @pl.when(pl.program_id(0) == 0)
    def _():
        for r in range(xs):
            for s in range(zs // 2):
                pick = [
                    lax.rem(where_ref[2] + r, xs) * zs + lax.bitwise_xor(where_ref[3], 2 * s + odd)
                    for odd in range(2)
                ]
                for i in range(size):
                    at = ((i * xs + r) * zs + 2 * s) * ROWS
                    for t in range(tiles):
                        if t < whole:
                            tile = core * whole + t
                        elif t < 2 * whole:
                            tile = (1 - core) * whole + t - whole
                        else:
                            tile = t
                        pair = jnp.concatenate([x_ref[q, i, tile] for q in pick], axis=0)
                        lhs[at : at + 2 * ROWS, t * LANES : (t + 1) * LANES] = pair

    total = jnp.zeros((lhs.shape[0], own_ref.shape[3]), F32)
    for part in range(2):
        total += jnp.dot(lhs[:, :main], own_ref[0, part, :main], preferred_element_type=F32)
        total += jnp.dot(lhs[:, main : 2 * main], other_ref[0, part, :main], preferred_element_type=F32)
        own, other = own_ref[0, part, main:], other_ref[0, part, main:]
        edge = jnp.where(core == 0, jnp.concatenate([own, other], axis=0), jnp.concatenate([other, own], axis=0))
        total += jnp.dot(lhs[:, 2 * main : 2 * main + 2 * LEFT], edge, preferred_element_type=F32)
    return total


def ladder_kernel(xs, where_ref, x_ref, own_ref, other_ref, *refs):
    o_refs, lhs = refs[:-1], refs[-1]
    total = ladder_block(xs, where_ref, x_ref, own_ref, other_ref, lhs)
    size, zs, block = x_ref.shape[1], x_ref.shape[0] // xs, total.shape[1]
    total = total.reshape(size, xs, zs, ROWS, block)
    at = pl.ds(pl.multiple_of(pl.program_id(0) * block, block), block)
    for k, o_ref in enumerate(o_refs):
        for i in range(size):
            o_ref[:, i, :, :, at] = total[i, :, :, k * COPIES : (k + 1) * COPIES, :]


def whole_kernel(xs, where_ref, x_ref, own_ref, other_ref, o_ref, f_ref, lhs, most):
    total = ladder_block(xs, where_ref, x_ref, own_ref, other_ref, lhs)
    block = total.shape[1]
    total = total.reshape(o_ref.shape[0], ROWS, block)
    step = pl.program_id(0)
    at = pl.ds(pl.multiple_of(step * block, block), block)
    o_ref[:, :, at] = total
    top = jnp.max(jnp.abs(total), axis=0)

    @pl.when(step == 0)
    def _():
        most[...] = top

    @pl.when(step > 0)
    def _():
        most[...] = jnp.maximum(most[...], top)

    @pl.when(step == pl.num_programs(0) - 1)
    def _():
        left = jnp.max(most[...])
        factors, inverses = [], []
        for _ in range(3):
            factor, inverse = jnp.float32(1), jnp.float32(1)
            for power in (7, 4, 2, 1):
                small = left * float(2**power) <= 16384.0
                grow = jnp.where(small, float(2**power), 1.0)
                left, factor = left * grow, factor * grow
                inverse = inverse * jnp.where(small, 2.0**-power, 1.0)
            factors.append(factor)
            inverses.append(inverse)
        lane = lax.broadcasted_iota(jnp.int32, f_ref.shape, 1)
        out = jnp.zeros(f_ref.shape, F32)
        for n, value in enumerate([factors[0] * factors[1] * factors[2]] + inverses):
            out = jnp.where(lane == n, value, out)
        f_ref[...] = out


def ladder(panels, own, other, where, xs, ys, whole=False):
    chips, size, tiles = panels.shape[:3]
    zs = chips // xs
    blocks, _, padded, block = own.shape
    count = blocks * block
    scratch = [pltpu.VMEM((size * chips * ROWS, tiles * LANES), BF)]
    if whole:
        shapes = [(chips, ROWS, count), (8, LANES)]
        scratch.append(pltpu.VMEM((ROWS, block), F32))
    else:
        shapes = [(xs, size, zs, COPIES, count)] * ys
    kernel = whole_kernel if whole else ladder_kernel
    return pl.pallas_call(
        lambda *refs: kernel(xs, *refs),
        grid_spec=pltpu.PrefetchScalarGridSpec(
            num_scalar_prefetch=1,
            grid=(blocks,),
            in_specs=[
                pl.BlockSpec(panels.shape, lambda n, where: (0, 0, 0, 0, 0), pipeline_mode=pl.Buffered(1)),
                pl.BlockSpec((1, 2, padded, block), lambda n, where: (n, 0, 0, 0)),
                pl.BlockSpec((1, 2, padded, block), lambda n, where: (n, 0, 0, 0)),
            ],
            out_specs=[pl.BlockSpec(shape, lambda n, where, rank=len(shape): (0,) * rank) for shape in shapes],
            scratch_shapes=scratch,
        ),
        out_shape=[jax.ShapeDtypeStruct(shape, F32) for shape in shapes],
        compiler_params=params(LADDER_MIB),
        cost_estimate=pl.CostEstimate(
            flops=4 * size * chips * ROWS * tiles * LANES * count,
            bytes_accessed=size * 3_000_000 + 9_000_000,
            transcendentals=0,
        ),
    )(where, panels, own, other)


def encode(partial, factors):
    count = partial.shape[2]
    lane = lax.broadcasted_iota(jnp.int32, partial.shape, 2)
    coded = partial * factors[0, 0]
    for n in range(3):
        coded = jnp.where(lane == count - 1 - n, factors[0, 1 + n], coded)
    return coded.astype(jnp.float16)


def decode(coded):
    wide = coded.astype(F32)
    count = wide.shape[2]
    inverse = wide[:, :1, count - 1 :] * wide[:, :1, count - 2 : count - 1] * wide[:, :1, count - 3 : count - 2]
    return jnp.sum(wide * inverse, axis=0)


def further(block, axis, hops):
    if hops == 0:
        return block
    size = lax.axis_size(axis)
    return lax.ppermute(block, axis, [(i, (i + hops) % size) for i in range(size)])


def update_kernel(place_ref, g_ref, col_ref, pair_ref, ea_ref, eb_ref, o_ref, slots_of):
    parts, rows, count = slots_of.shape
    done = rows - COPIES
    for k in range(parts):
        slots_of[lax.rem(place_ref[0] + parts - k, parts), :done] = g_ref[k, :done]
    last = g_ref[0, rows:]
    for k in range(1, parts):
        last = last + g_ref[k, rows:]
    for k in range(parts):
        slots_of[k, done:] = last[k * COPIES : (k + 1) * COPIES]
    total = slots_of[...].reshape(parts * rows, count)
    slots = parts * rows
    hi = total.astype(BF).astype(F32)
    mid = (total - hi).astype(BF).astype(F32)
    low = total - hi - mid
    split = jnp.concatenate([hi, mid, low], axis=0).astype(BF)
    row = lax.broadcasted_iota(jnp.int32, (count, col_ref.shape[1]), 0)
    pick = (row == col_ref[...]).astype(F32).astype(BF)
    wide = jnp.dot(split, pick, preferred_element_type=F32)
    residual = wide[:slots] + wide[slots : 2 * slots] + wide[2 * slots :]
    denominator = pair_ref[...] - ea_ref[...] - eb_ref[...]
    o_ref[...] = residual / denominator


def body(amps, integrals, slot_pair, occ_energy, virt_energy):
    slots = amps.shape[0]
    window = virt_energy.shape[0]
    xs, zs, ys = lax.axis_size("x"), lax.axis_size("z"), lax.axis_size("y")
    local_rows = window // ys
    one, two = unique_pairs(window)
    count = one.shape[1]
    where = jnp.stack([lax.axis_index(axis).astype(jnp.int32) for axis in ("c", "y", "x", "z")])
    plain = where * jnp.asarray([1, 0, 0, 0], jnp.int32)
    place = lax.axis_index("y").astype(jnp.int32)
    own = fold(integrals.T, jnp.asarray(one), jnp.asarray(two))
    other = lax.ppermute(own, "c", [(0, 1), (1, 0)])
    done = []
    start = 0
    for chunk, size in enumerate(SIZES):
        final = chunk == len(SIZES) - 1
        flat = flatten(amps, start, size, plain if final else where, xs, zs)
        start += size
        panels = lax.all_to_all(flat, ("x", "z"), 0, 0, tiled=True)
        partial = ladder(panels, own, other, plain if final else where, xs, ys, final)
        if final:
            coded = encode(*partial)
            coded = lax.all_to_all(coded, ("x", "z"), 0, 0, tiled=True)
            last = decode(coded)
            continue
        partial = [further(block, "y", k) for k, block in enumerate(partial)]
        partial = [sum((block[r] for block in partial[1:]), partial[0][r]) for r in range(xs)]
        partial = [further(block, "x", r) for r, block in enumerate(partial)]
        done.append(sum(partial[1:], partial[0]))
    mine = jnp.concatenate(done, axis=0)
    apart = [mine[:, s] for s in range(zs)]
    apart = [apart[0]] + [
        lax.ppermute(apart[s], "z", [(i, i ^ s) for i in range(zs)]) for s in range(1, zs)
    ]
    mine = sum(apart[1:], apart[0])
    mine = mine.reshape(-1, count)
    mine = jnp.concatenate([jnp.pad(mine, ((0, COPIES), (0, 0))), last], axis=0)
    everyone = jnp.stack([further(mine, "y", k) for k in range(ys)])

    pair_sum, filled = pair_energy(slot_pair, occ_energy)
    first = place * local_rows
    a = jnp.repeat(first + jnp.arange(local_rows, dtype=jnp.int32), window)
    b = jnp.tile(jnp.arange(window, dtype=jnp.int32), local_rows)
    low, high = jnp.minimum(a, b), jnp.maximum(a, b)
    column = low * window - low * (low - 1) // 2 + high - low
    wide = local_rows * window
    full = -(-wide // LANES) * LANES
    column = jnp.pad(column, (0, full - wide), constant_values=-1)[None]
    local_energy = lax.dynamic_slice_in_dim(virt_energy, first, local_rows)
    ea = jnp.pad(jnp.repeat(local_energy, window), (0, full - wide))[None]
    eb = jnp.pad(jnp.tile(virt_energy, local_rows), (0, full - wide))[None]
    update = pl.pallas_call(
        update_kernel,
        in_specs=[pl.BlockSpec(memory_space=pltpu.SMEM)] + [pl.BlockSpec(memory_space=pltpu.VMEM)] * 5,
        out_shape=jax.ShapeDtypeStruct((slots, full), F32),
        scratch_shapes=[pltpu.VMEM((ys, slots // ys, count), F32)],
        compiler_params=params(24),
    )(place[None], everyone, column, pair_sum[:, None], ea, eb)
    update = update[:, :wide].reshape(slots, local_rows, window)
    return jnp.where(filled[:, None, None], update, jnp.zeros_like(update))


SIZES = (2, 1, 1)


def solution(mesh):
    grid = Mesh(mesh.devices.reshape(8, 4, 2, mesh.shape["virt"]), ("z", "x", "c", "y"))
    placed = (P(("z", "x", "c"), "y", None), P(None, ("y", "z", "x", "c")), P(("z", "x", "c")), P(), P())
    return jax.shard_map(
        body, mesh=grid, in_specs=placed, out_specs=P(("z", "x", "c"), "y", None), check_vma=False
    )
```

```python
import jax
import jax.numpy as jnp
import numpy as np
from jax import lax
from jax.experimental import pallas as pl
from jax.experimental.pallas import tpu as pltpu
from jax.sharding import Mesh, PartitionSpec as P

ROWS = 8
LEFT = 16
COPIES = 2
MIB = 36
LANES = 128
BF = jnp.bfloat16
F32 = jnp.float32


def params(mib):
    return pltpu.CompilerParams(vmem_limit_bytes=mib * 1024 * 1024)


def pair_energy(slot_pair, occ_energy):
    nocc_count = occ_energy.shape[0]
    orbital = jnp.arange(nocc_count, dtype=jnp.int32)
    starts_row = orbital * nocc_count - orbital * (orbital - 1) // 2
    row_index = jnp.sum((starts_row[None, 1:] <= slot_pair[:, None]).astype(jnp.int32), axis=1)
    same_row = orbital[None, :] == row_index[:, None]
    row_start = jnp.sum(jnp.where(same_row, starts_row[None, :], 0), axis=1)
    column_index = slot_pair - row_start + row_index
    first_energy = jnp.sum(
        jnp.where(same_row, occ_energy[None, :], jnp.zeros_like(occ_energy)[None, :]), axis=1
    )
    same_column = orbital[None, :] == column_index[:, None]
    second_energy = jnp.sum(
        jnp.where(same_column, occ_energy[None, :], jnp.zeros_like(occ_energy)[None, :]), axis=1
    )
    return (first_energy + second_energy, slot_pair >= 0)


def unique_pairs(window):
    a, b = np.triu_indices(window)
    count = -(-a.size // 256) * 256
    one = np.full((1, count), -1, np.int32)
    two = np.full((1, count), -1, np.int32)
    one[0, : a.size] = a * window + b
    two[0, : a.size] = b * window + a
    return one, two


def flatten_kernel(xs, zs, width, where_ref, x_ref, o_ref, rows, flat):
    parts, count, inner = x_ref.shape[0], x_ref.shape[3], x_ref.shape[4]
    for k in range(0, inner, LANES):
        part = min(LANES, inner - k)
        for s in range(ROWS):
            rows[k // LANES, pl.ds(s * count, count), :part] = x_ref[
                lax.rem(where_ref[1] + s // COPIES, parts), 0, s % COPIES, :, k : k + part
            ].astype(F32)
    for c in range(count):
        for k in range(0, inner, LANES):
            part = min(LANES, inner - k)
            piece = rows[k // LANES, pl.ds(c, ROWS, stride=count), :]
            flat[:, c * inner + k : c * inner + k + part] = piece[:, :part]
    flat[:, count * inner :] = jnp.zeros((ROWS, flat.shape[1] - count * inner), F32)
    whole = width // LANES
    main = whole * LANES
    lane = lax.broadcasted_iota(jnp.int32, (ROWS, LANES), 1)
    for z in range(zs):
        for x in range(xs):
            base = (z * xs + x) * 2 * width
            q = x * zs + z
            for half in range(2):
                for t in range(whole):
                    at = base + half * width + t * LANES
                    o_ref[q, 0, half * whole + t] = flat[:, at : at + LANES].astype(BF)
            low, high = base + main, base + width + main - LEFT
            edge = jnp.where(lane < LEFT, flat[:, low : low + LANES], flat[:, high : high + LANES])
            o_ref[q, 0, 2 * whole] = edge.astype(BF)


def flatten(amps, start, size, where, xs, zs):
    slots, count, inner = amps.shape
    width = count * inner // (xs * zs * 2)
    tiles = width // LANES * 2 + 1
    parts = ROWS // COPIES
    view = amps.reshape(parts, slots // ROWS, COPIES, count, inner)
    return pl.pallas_call(
        lambda *refs: flatten_kernel(xs, zs, width, *refs),
        grid_spec=pltpu.PrefetchScalarGridSpec(
            num_scalar_prefetch=1,
            grid=(size,),
            in_specs=[
                pl.BlockSpec((parts, 1, COPIES, count, inner), lambda i, where: (0, start + i, 0, 0, 0))
            ],
            out_specs=pl.BlockSpec((xs * zs, 1, tiles, ROWS, LANES), lambda i, where: (0, i, 0, 0, 0)),
            scratch_shapes=[
                pltpu.VMEM((-(-inner // LANES), ROWS * count, LANES), F32),
                pltpu.VMEM((ROWS, count * inner + 2 * LANES), F32),
            ],
        ),
        out_shape=jax.ShapeDtypeStruct((xs * zs, size, tiles, ROWS, LANES), BF),
        compiler_params=params(60 if start == 0 else MIB),
        cost_estimate=pl.CostEstimate(flops=0, bytes_accessed=8_000_000, transcendentals=0),
    )(where, view)


def fold_kernel(one_ref, two_ref, b_ref, o_ref):
    width, full = b_ref.shape
    row = lax.broadcasted_iota(jnp.int32, (full, one_ref.shape[1]), 0)
    pick = (row == one_ref[...]).astype(F32) + (row == two_ref[...]).astype(F32)
    both = jnp.dot(b_ref[...], pick.astype(BF), preferred_element_type=F32)
    rest = o_ref.shape[2] - width
    both = jnp.concatenate([both, jnp.zeros((rest, both.shape[1]), F32)], axis=0)
    hi = both.astype(BF)
    o_ref[0, 0] = hi
    o_ref[0, 1] = (both - hi.astype(F32)).astype(BF)


def fold(columns, one, two):
    width, full = columns.shape
    padded = width // LANES * LANES + LEFT
    count, block = one.shape[1], 256
    return pl.pallas_call(
        fold_kernel,
        grid=(count // block,),
        in_specs=[
            pl.BlockSpec((1, block), lambda i: (0, i)),
            pl.BlockSpec((1, block), lambda i: (0, i)),
            pl.BlockSpec((width, full), lambda i: (0, 0), pipeline_mode=pl.Buffered(1)),
        ],
        out_specs=pl.BlockSpec((1, 2, padded, block), lambda i: (i, 0, 0, 0)),
        out_shape=jax.ShapeDtypeStruct((count // block, 2, padded, block), BF),
        compiler_params=params(MIB),
        cost_estimate=pl.CostEstimate(
            flops=2 * width * full * count, bytes_accessed=10_000_000, transcendentals=0
        ),
    )(one, two, columns)


def ladder_block(xs, where_ref, x_ref, own_ref, other_ref, lhs):
    chips, size, tiles = x_ref.shape[:3]
    zs = chips // xs
    whole = tiles // 2
    main = whole * LANES
    core = where_ref[0]

    @pl.when(pl.program_id(0) == 0)
    def _():
        for r in range(xs):
            for s in range(zs // 2):
                pick = [
                    lax.rem(where_ref[2] + r, xs) * zs + lax.bitwise_xor(where_ref[3], 2 * s + odd)
                    for odd in range(2)
                ]
                for i in range(size):
                    at = ((i * xs + r) * zs + 2 * s) * ROWS
                    for t in range(tiles):
                        if t < whole:
                            tile = core * whole + t
                        elif t < 2 * whole:
                            tile = (1 - core) * whole + t - whole
                        else:
                            tile = t
                        pair = jnp.concatenate([x_ref[q, i, tile] for q in pick], axis=0)
                        lhs[at : at + 2 * ROWS, t * LANES : (t + 1) * LANES] = pair

    total = jnp.zeros((lhs.shape[0], own_ref.shape[3]), F32)
    for part in range(2):
        total += jnp.dot(lhs[:, :main], own_ref[0, part, :main], preferred_element_type=F32)
        total += jnp.dot(lhs[:, main : 2 * main], other_ref[0, part, :main], preferred_element_type=F32)
        own, other = own_ref[0, part, main:], other_ref[0, part, main:]
        edge = jnp.where(core == 0, jnp.concatenate([own, other], axis=0), jnp.concatenate([other, own], axis=0))
        total += jnp.dot(lhs[:, 2 * main : 2 * main + 2 * LEFT], edge, preferred_element_type=F32)
    return total


def ladder_kernel(xs, where_ref, x_ref, own_ref, other_ref, *refs):
    o_refs, lhs = refs[:-1], refs[-1]
    total = ladder_block(xs, where_ref, x_ref, own_ref, other_ref, lhs)
    size, zs, block = x_ref.shape[1], x_ref.shape[0] // xs, total.shape[1]
    total = total.reshape(size, xs, zs, ROWS, block)
    at = pl.ds(pl.multiple_of(pl.program_id(0) * block, block), block)
    for k, o_ref in enumerate(o_refs):
        for i in range(size):
            o_ref[:, i, :, :, at] = total[i, :, :, k * COPIES : (k + 1) * COPIES, :]


def whole_kernel(xs, where_ref, x_ref, own_ref, other_ref, o_ref, f_ref, lhs, most):
    total = ladder_block(xs, where_ref, x_ref, own_ref, other_ref, lhs)
    block = total.shape[1]
    total = total.reshape(o_ref.shape[0], ROWS, block)
    step = pl.program_id(0)
    at = pl.ds(pl.multiple_of(step * block, block), block)
    o_ref[:, :, at] = total
    top = jnp.max(jnp.abs(total), axis=0)

    @pl.when(step == 0)
    def _():
        most[...] = top

    @pl.when(step > 0)
    def _():
        most[...] = jnp.maximum(most[...], top)

    @pl.when(step == pl.num_programs(0) - 1)
    def _():
        left = jnp.max(most[...])
        factors, inverses = [], []
        for _ in range(3):
            factor, inverse = jnp.float32(1), jnp.float32(1)
            for power in (7, 4, 2, 1):
                small = left * float(2**power) <= 16384.0
                grow = jnp.where(small, float(2**power), 1.0)
                left, factor = left * grow, factor * grow
                inverse = inverse * jnp.where(small, 2.0**-power, 1.0)
            factors.append(factor)
            inverses.append(inverse)
        lane = lax.broadcasted_iota(jnp.int32, f_ref.shape, 1)
        out = jnp.zeros(f_ref.shape, F32)
        for n, value in enumerate([factors[0] * factors[1] * factors[2]] + inverses):
            out = jnp.where(lane == n, value, out)
        f_ref[...] = out


def ladder(panels, own, other, where, xs, ys, whole=False):
    chips, size, tiles = panels.shape[:3]
    zs = chips // xs
    blocks, _, padded, block = own.shape
    count = blocks * block
    scratch = [pltpu.VMEM((size * chips * ROWS, tiles * LANES), BF)]
    if whole:
        shapes = [(chips, ROWS, count), (8, LANES)]
        scratch.append(pltpu.VMEM((ROWS, block), F32))
    else:
        shapes = [(xs, size, zs, COPIES, count)] * ys
    kernel = whole_kernel if whole else ladder_kernel
    return pl.pallas_call(
        lambda *refs: kernel(xs, *refs),
        grid_spec=pltpu.PrefetchScalarGridSpec(
            num_scalar_prefetch=1,
            grid=(blocks,),
            in_specs=[
                pl.BlockSpec(panels.shape, lambda n, where: (0, 0, 0, 0, 0), pipeline_mode=pl.Buffered(1)),
                pl.BlockSpec((1, 2, padded, block), lambda n, where: (n, 0, 0, 0)),
                pl.BlockSpec((1, 2, padded, block), lambda n, where: (n, 0, 0, 0)),
            ],
            out_specs=[pl.BlockSpec(shape, lambda n, where, rank=len(shape): (0,) * rank) for shape in shapes],
            scratch_shapes=scratch,
        ),
        out_shape=[jax.ShapeDtypeStruct(shape, F32) for shape in shapes],
        compiler_params=params(MIB),
        cost_estimate=pl.CostEstimate(
            flops=4 * size * chips * ROWS * tiles * LANES * count,
            bytes_accessed=size * 3_000_000 + 9_000_000,
            transcendentals=0,
        ),
    )(where, panels, own, other)


def encode(partial, factors):
    count = partial.shape[2]
    lane = lax.broadcasted_iota(jnp.int32, partial.shape, 2)
    coded = partial * factors[0, 0]
    for n in range(3):
        coded = jnp.where(lane == count - 1 - n, factors[0, 1 + n], coded)
    return coded.astype(jnp.float16)


def decode(coded):
    wide = coded.astype(F32)
    count = wide.shape[2]
    inverse = wide[:, :1, count - 1 :] * wide[:, :1, count - 2 : count - 1] * wide[:, :1, count - 3 : count - 2]
    return jnp.sum(wide * inverse, axis=0)


def further(block, axis, hops):
    if hops == 0:
        return block
    size = lax.axis_size(axis)
    return lax.ppermute(block, axis, [(i, (i + hops) % size) for i in range(size)])


def update_kernel(place_ref, g_ref, col_ref, pair_ref, ea_ref, eb_ref, o_ref, slots_of):
    parts, rows, count = slots_of.shape
    done = rows - COPIES
    for k in range(parts):
        slots_of[lax.rem(place_ref[0] + parts - k, parts), :done] = g_ref[k, :done]
    last = g_ref[0, rows:]
    for k in range(1, parts):
        last = last + g_ref[k, rows:]
    for k in range(parts):
        slots_of[k, done:] = last[k * COPIES : (k + 1) * COPIES]
    total = slots_of[...].reshape(parts * rows, count)
    slots = parts * rows
    hi = total.astype(BF).astype(F32)
    mid = (total - hi).astype(BF).astype(F32)
    low = total - hi - mid
    split = jnp.concatenate([hi, mid, low], axis=0).astype(BF)
    row = lax.broadcasted_iota(jnp.int32, (count, col_ref.shape[1]), 0)
    pick = (row == col_ref[...]).astype(F32).astype(BF)
    wide = jnp.dot(split, pick, preferred_element_type=F32)
    residual = wide[:slots] + wide[slots : 2 * slots] + wide[2 * slots :]
    denominator = pair_ref[...] - ea_ref[...] - eb_ref[...]
    o_ref[...] = residual / denominator


def body(amps, integrals, slot_pair, occ_energy, virt_energy):
    slots = amps.shape[0]
    window = virt_energy.shape[0]
    xs, zs, ys = lax.axis_size("x"), lax.axis_size("z"), lax.axis_size("y")
    local_rows = window // ys
    one, two = unique_pairs(window)
    count = one.shape[1]
    where = jnp.stack([lax.axis_index(axis).astype(jnp.int32) for axis in ("c", "y", "x", "z")])
    plain = where * jnp.asarray([1, 0, 0, 0], jnp.int32)
    place = lax.axis_index("y").astype(jnp.int32)
    own = fold(integrals.T, jnp.asarray(one), jnp.asarray(two))
    other = lax.ppermute(own, "c", [(0, 1), (1, 0)])
    done = []
    start = 0
    for chunk, size in enumerate(SIZES):
        final = chunk == len(SIZES) - 1
        flat = flatten(amps, start, size, plain if final else where, xs, zs)
        start += size
        panels = lax.all_to_all(flat, ("x", "z"), 0, 0, tiled=True)
        partial = ladder(panels, own, other, plain if final else where, xs, ys, final)
        if final:
            coded = encode(*partial)
            coded = lax.all_to_all(coded, ("x", "z"), 0, 0, tiled=True)
            last = decode(coded)
            continue
        partial = [further(block, "y", k) for k, block in enumerate(partial)]
        partial = [sum((block[r] for block in partial[1:]), partial[0][r]) for r in range(xs)]
        partial = [further(block, "x", r) for r, block in enumerate(partial)]
        done.append(sum(partial[1:], partial[0]))
    mine = jnp.concatenate(done, axis=0)
    mine = mine.reshape(-1, zs // 2, 2, COPIES, count)
    odd = lax.ppermute(mine[:, :, 1], "z", [(i, i ^ 1) for i in range(zs)])
    mine = mine[:, :, 0] + odd
    apart = [mine[:, 0]] + [
        lax.ppermute(mine[:, s], "z", [(i, i ^ (2 * s)) for i in range(zs)]) for s in range(1, zs // 2)
    ]
    mine = sum(apart[1:], apart[0])
    mine = mine.reshape(-1, count)
    mine = jnp.concatenate([jnp.pad(mine, ((0, COPIES), (0, 0))), last], axis=0)
    everyone = jnp.stack([further(mine, "y", k) for k in range(ys)])

    pair_sum, filled = pair_energy(slot_pair, occ_energy)
    first = place * local_rows
    a = jnp.repeat(first + jnp.arange(local_rows, dtype=jnp.int32), window)
    b = jnp.tile(jnp.arange(window, dtype=jnp.int32), local_rows)
    low, high = jnp.minimum(a, b), jnp.maximum(a, b)
    column = low * window - low * (low - 1) // 2 + high - low
    wide = local_rows * window
    full = -(-wide // LANES) * LANES
    column = jnp.pad(column, (0, full - wide), constant_values=-1)[None]
    local_energy = lax.dynamic_slice_in_dim(virt_energy, first, local_rows)
    ea = jnp.pad(jnp.repeat(local_energy, window), (0, full - wide))[None]
    eb = jnp.pad(jnp.tile(virt_energy, local_rows), (0, full - wide))[None]
    update = pl.pallas_call(
        update_kernel,
        in_specs=[pl.BlockSpec(memory_space=pltpu.SMEM)] + [pl.BlockSpec(memory_space=pltpu.VMEM)] * 5,
        out_shape=jax.ShapeDtypeStruct((slots, full), F32),
        scratch_shapes=[pltpu.VMEM((ys, slots // ys, count), F32)],
        compiler_params=params(MIB),
    )(place[None], everyone, column, pair_sum[:, None], ea, eb)
    update = update[:, :wide].reshape(slots, local_rows, window)
    return jnp.where(filled[:, None, None], update, jnp.zeros_like(update))


SIZES = (2, 1, 1)


def solution(mesh):
    grid = Mesh(mesh.devices.reshape(8, 4, 2, mesh.shape["virt"]), ("z", "x", "c", "y"))
    placed = (P(("z", "x", "c"), "y", None), P(None, ("y", "z", "x", "c")), P(("z", "x", "c")), P(), P())
    return jax.shard_map(
        body, mesh=grid, in_specs=placed, out_specs=P(("z", "x", "c"), "y", None), check_vma=False
    )
```
